32 devices in a mesh: tm: 2 (over core), height: 16 (over z, y, x).
Axes of the slice: x: 2, y: 2, z: 4, core: 2. Of those that a mesh axis runs over, the one named last changes fastest.
Arguments:
- clip: bfloat16 [4, 128, 48, 256], P('tm', 'height'), may hold values from -6 to 6
- teacher: bfloat16 [4, 128, 48, 256], P('tm', 'height'), may hold values from -6 to 6
- kernel_one: bfloat16 [6912, 256], P('height'), may hold values from -0.078125 to 0.078125
- kernel_two: bfloat16 [6912, 256], P('height'), may hold values from -0.078125 to 0.078125
Outputs:
- student: bfloat16 [4, 128, 48, 256], P('tm', 'height')
- grad_one: float32 [6912, 256], P('height')
- grad_two: float32 [6912, 256], P('height')
The draws below stay inside these ranges and needn't reach their ends.
All inputs are finite; a program needn't handle non-finite values.
Results may differ from the reference program's by a relative error of at most 0.013.
Values may be sent and summed in bfloat16 or wider, within the bound.
No kernel may reach another device: no remote copies, remote signals or barrier semaphores. Data moves between devices by JAX's collectives and lax.ppermute only.
A program may use at most 128 MiB of HBM per device.

```python
import jax
import jax.numpy as jnp
from jax import lax

C = 256
W = 48
FRAMES = 4
HGT = 128
CLIPS = 1


def steps_of(rng, dims, shards, low, high):
    level, own = 1.0, jax.random.fold_in(rng, 6)
    for dim, parts in shards:
        draws = jnp.exp(jax.random.uniform(jax.random.fold_in(own, dim), (parts,), jnp.float32, low / len(shards), high / len(shards)))
        level = level * jnp.repeat(draws, dims[dim] // parts).reshape([-1 if axis == dim else 1 for axis in range(len(dims))])
    return level


def centred(own_key, extent, deviation, bound, cuts=(), kind=jnp.bfloat16):
    loudness = steps_of(own_key, extent, cuts, -0.22, 0.18) if cuts else 1.0
    array = jax.random.normal(own_key, extent, jnp.float32) * deviation * loudness
    return jnp.minimum(jnp.maximum(array, -bound), bound).astype(kind)


def setup_inputs(seed: int = 0) -> dict:
    arg_keys = jax.random.split(jax.random.key(seed), 5)
    return {
        "clip": centred(arg_keys[0], (FRAMES, CLIPS * HGT, W, C), 1.0, 6.0, ((0, 2), (1, 16))),
        "teacher": centred(arg_keys[1], (FRAMES, CLIPS * HGT, W, C), 1.0, 6.0, ((0, 2), (1, 16))),
        "kernel_one": centred(arg_keys[2], (27 * C, C), (27 * C) ** -0.5, 0.078125, ((0, 16),)),
        "kernel_two": centred(arg_keys[3], (27 * C, C), (27 * C) ** -0.5, 0.078125, ((0, 16),)),
    }


def tap_offsets():
    return [(t_off, h_off, w_off) for t_off in range(3) for h_off in range(3) for w_off in range(3)]

def frame_patches(padded, frame_at, causal):
    window = lax.dynamic_slice_in_dim(padded, frame_at, 3, 0)
    pieces = []
    for t_off, h_off, w_off in tap_offsets():
        if causal:
            pieces.append(window[t_off, h_off:h_off + HGT, w_off:w_off + W])
        else:
            pieces.append(window[2 - t_off, 2 - h_off:2 - h_off + HGT, 2 - w_off:2 - w_off + W])
    return jnp.stack(pieces, axis=2).reshape(HGT * W, 27 * C)

def conv_forward(values, kernel):
    padded = jnp.pad(values, ((2, 0), (1, 1), (1, 1), (0, 0)))

    def one_frame(frame_at):
        return jnp.dot(frame_patches(padded, frame_at, True), kernel, preferred_element_type=jnp.float32)
    return lax.map(one_frame, jnp.arange(FRAMES, dtype=jnp.int32))

def kernel_grad(values, grads):
    padded = jnp.pad(values, ((2, 0), (1, 1), (1, 1), (0, 0)))

    def add_frame(total, frame_at):
        patches = frame_patches(padded, frame_at, True)
        term = lax.dot_general(patches, grads[frame_at], (((0,), (0,)), ((), ())), preferred_element_type=jnp.float32)
        return (total + term, None)
    total, unused = lax.scan(add_frame, jnp.zeros((27 * C, C), jnp.float32), jnp.arange(FRAMES, dtype=jnp.int32))
    return total

def input_grad(grads, kernel):
    padded = jnp.pad(grads.reshape(FRAMES, HGT, W, C), ((0, 2), (1, 1), (1, 1), (0, 0)))
    kernel_taps = kernel.astype(jnp.float32).reshape(27, C, C)

    def one_frame(frame_at):
        patches = frame_patches(padded, frame_at, False).reshape(HGT * W, 27, C).astype(jnp.float32)
        return jnp.einsum('rkc,kdc->rd', patches, kernel_taps)
    return lax.map(one_frame, jnp.arange(FRAMES, dtype=jnp.int32))

def one_clip(clip, teacher, kernel_one, kernel_two):
    pre_act = conv_forward(clip, kernel_one)
    hidden = jax.nn.silu(pre_act).astype(jnp.bfloat16)
    branch = conv_forward(hidden.reshape(FRAMES, HGT, W, C), kernel_two)
    output = clip.reshape(FRAMES, HGT * W, C).astype(jnp.float32) + branch
    student = output.astype(jnp.bfloat16).reshape(FRAMES, HGT, W, C)
    factor = 1.0 / jnp.sqrt(jnp.float32(CLIPS * FRAMES * HGT * W))
    grad_out = ((output - teacher.reshape(FRAMES, HGT * W, C).astype(jnp.float32)) * factor).astype(jnp.bfloat16)
    grad_two = kernel_grad(hidden.reshape(FRAMES, HGT, W, C), grad_out)
    grad_hidden = input_grad(grad_out, kernel_two)
    sigmoid_pre = jax.nn.sigmoid(pre_act)
    grad_pre = (grad_hidden * sigmoid_pre * (1.0 + pre_act * (1.0 - sigmoid_pre))).astype(jnp.bfloat16)
    grad_one = kernel_grad(clip, grad_pre)
    return (student, grad_one, grad_two)

def reference(clip, teacher, kernel_one, kernel_two):
    clips_first = jnp.transpose(clip.reshape(FRAMES, CLIPS, HGT, W, C), (1, 0, 2, 3, 4))
    teachers_first = jnp.transpose(teacher.reshape(FRAMES, CLIPS, HGT, W, C), (1, 0, 2, 3, 4))

    def add_clip(totals, index):
        student, grad_one, grad_two = one_clip(clips_first[index], teachers_first[index], kernel_one, kernel_two)
        return ((totals[0] + grad_one, totals[1] + grad_two), student)
    zeros = jnp.zeros((27 * C, C), jnp.float32)
    totals, students = lax.scan(add_clip, (zeros, zeros), jnp.arange(CLIPS, dtype=jnp.int32))
    student = jnp.transpose(students, (1, 0, 2, 3, 4)).reshape(FRAMES, CLIPS * HGT, W, C)
    return (student, totals[0], totals[1])
```

```python
import functools
import math

import jax
import jax.numpy as jnp
from jax import lax
from jax.experimental import pallas as pl
from jax.experimental.pallas import tpu as pltpu
from jax.sharding import PartitionSpec as P


BOTH = ("tm", "height")
BF16 = jnp.bfloat16
F32 = jnp.float32
VMEM_LIMIT = 56 * 1024 * 1024
TAPS = 3


def step_bits(blocks):
    bits = blocks.bit_length() - 1
    assert 1 << bits == blocks and bits >= 4, "height size"
    high = list(range(bits - 1, 1, -1))
    return high + [0, 1], [high[1], high[0]] + high[2:] + [1, 0]


def relative_masks(order):
    return [sum(((r >> k) & 1) << bit for k, bit in enumerate(order)) for r in range(1 << len(order))]


def step_pairs(frames_axis, blocks, step):
    orders = step_bits(blocks)
    return [
        (t * blocks + h, t * blocks + (h ^ (1 << orders[t % 2][step])))
        for t in range(frames_axis)
        for h in range(blocks)
    ]


def core_pairs(frames_axis):
    return [(t, t ^ 1) for t in range(frames_axis)]


def shifted(value, axis, by):
    count = lax.axis_size(axis)
    return lax.ppermute(value, axis, [(i, i + by) for i in range(count) if 0 <= i + by < count])


def gather_kernel(shard, core):
    frames_axis, blocks = lax.axis_size("tm"), lax.axis_size("height")
    half = shard.shape[1] // 2
    steps = blocks.bit_length() - 1
    near = lax.dynamic_slice(shard, (0, core * half), (shard.shape[0], half))[None]
    for step in range(steps - 1):
        got = lax.ppermute(near, BOTH, step_pairs(frames_axis, blocks, step))
        near = jnp.concatenate([near, got], axis=0)
    far = lax.ppermute(near, BOTH, step_pairs(frames_axis, blocks, steps - 1))
    near_other = lax.ppermute(near, "tm", core_pairs(frames_axis))
    far_other = lax.ppermute(far, "tm", core_pairs(frames_axis))
    return near, far, near_other, far_other


def total(first, second):
    return first.astype(F32) + second.astype(F32)


def scatter_grad(keep, send, core):
    frames_axis, blocks = lax.axis_size("tm"), lax.axis_size("height")
    steps = blocks.bit_length() - 1
    here, came = keep, lax.ppermute(send, "tm", core_pairs(frames_axis))
    count = blocks
    for step in reversed(range(steps)):
        count //= 2
        away = total(here[count:], came[count:]).astype(BF16)
        got = lax.ppermute(away, BOTH, step_pairs(frames_axis, blocks, step))
        here = total(here[:count], came[:count])
        if count > 4:
            here = here.astype(BF16)
        came = got
    own = total(here[0], came[0])
    group = 2
    while group < frames_axis:
        own = total(own, lax.ppermute(own, "tm", [(t, t ^ group) for t in range(frames_axis)]))
        group *= 2
    other = lax.ppermute(own, "tm", core_pairs(frames_axis))
    first = jnp.where(core == 0, own, other)
    second = jnp.where(core == 0, other, own)
    return jnp.concatenate([first, second], axis=1)


OWN, OTHER, KEEP, SEND, INFO = range(5)


def column_shift(value, by):
    width = value.shape[1]
    cols = lax.broadcasted_iota(jnp.int32, value.shape, 1)
    rolled = pltpu.roll(value, by % width, 1)
    return jnp.where((cols < by) if by > 0 else (cols >= width + by), 0.0, rolled)


def weight_copies(meta, parts, whole, sems):
    near, far, near_other, far_other = parts
    count, rows, half = near.shape
    core = meta[INFO, 0]
    copies = []
    for which, (low, high, side) in enumerate(((near, far, core), (near_other, far_other, 1 - core))):
        lanes = pl.ds(pl.multiple_of(side * half, half), half)
        for r in range(2 * count):
            source = (low if r < count else high).at[r % count]
            owner = meta[OWN + which, r]
            place = whole.at[pl.ds(pl.multiple_of(owner * rows, rows), rows), lanes]
            copies.append(pltpu.make_async_copy(source, place, sems.at[which, r]))
    return copies


def tap_rows(chans, a, b, c):
    first = ((a * TAPS + b) * TAPS + c) * chans
    return slice(first, first + chans)


def conv_block(frame_rows, weights, chans, forward):
    result = None
    order = [(a, b) for a in range(TAPS) for b in range(TAPS)]
    pieces = [frame_rows(a, b) for a, b in order]
    rows, width, _ = pieces[0].shape
    left = jnp.concatenate([piece.reshape(rows * width, chans) for piece in pieces], axis=1)
    for c in range(TAPS):
        blocks = [weights[tap_rows(chans, a, b, c), :] for a, b in order]
        if forward:
            part = jnp.dot(left, jnp.concatenate(blocks, axis=0), preferred_element_type=F32)
        else:
            part = lax.dot_general(
                left, jnp.concatenate(blocks, axis=1), (((1,), (1,)), ((), ())), preferred_element_type=F32
            )
        part = part.reshape(rows, width, chans)
        by = (1 - c) if forward else (c - 1)
        if by:
            part = column_shift(part, by)
        result = part if result is None else result + part
    return result


def frame_of(earlier, current, at, rows):
    held = earlier.shape[0]
    return earlier[at, rows] if at < held else current[at - held, rows]


def conv_one_kernel(meta, earlier, current, near, far, near_o, far_o, hidden, slope, weights, sems):
    copies = weight_copies(meta, (near, far, near_o, far_o), weights, sems)
    for copy in copies:
        copy.start()
    for copy in copies:
        copy.wait()
    frames, rows, _, chans = hidden.shape
    for t in range(frames):
        pre = conv_block(
            lambda a, b: frame_of(earlier, current, t + a, slice(b, b + rows)), weights, chans, True
        )
        gate = 1.0 / (1.0 + jnp.exp(-pre))
        value = (pre * gate).astype(BF16)
        row = lax.broadcasted_iota(jnp.int32, value.shape, 0)
        cut = jnp.logical_or(
            jnp.logical_and(row == 0, meta[INFO, 1] == 1), jnp.logical_and(row == rows - 1, meta[INFO, 2] == 1)
        )
        hidden[t] = jnp.where(cut, jnp.zeros_like(value), value)
        slope[t] = (gate * (1.0 + pre * (1.0 - gate)))[1 : rows - 1]


def conv_two_kernel(
    factor, meta, earlier, current, clip, teacher, near, far, near_o, far_o, student, dout, weights, sems
):
    copies = weight_copies(meta, (near, far, near_o, far_o), weights, sems)
    for copy in copies:
        copy.start()
    for copy in copies:
        copy.wait()
    frames, rows, _, chans = student.shape
    for t in range(frames):
        branch = conv_block(
            lambda a, b: frame_of(earlier, current, t + a, slice(b, b + rows)), weights, chans, True
        )
        output = clip[t].astype(F32) + branch
        student[t] = output.astype(BF16)
        dout[t] = ((output - teacher[t].astype(F32)) * factor).astype(BF16)


def weight_grad(meta, value_rows, grads, frames, rows, width, chans, stage, keep, send, sems):
    size = frames * rows * width
    wide = grads.astype(F32)
    moved = [
        (column_shift(wide, c - 1).astype(BF16) if c != 1 else grads).reshape(size, chans) for c in range(TAPS)
    ]
    count, depth, half = keep.shape
    core = meta[INFO, 0]
    copies = []
    done = 0
    for a in range(TAPS):
        for b in range(TAPS):
            turned = value_rows(a, b).reshape(size, chans).T
            for c in range(TAPS):
                at = tap_rows(chans, a, b, c)
                stage[at, :] = jnp.dot(turned, moved[c], preferred_element_type=F32).astype(BF16)
                while (done + 1) * depth <= at.stop and done < count:
                    for which, (to, side) in enumerate(((keep, core), (send, 1 - core))):
                        lanes = pl.ds(pl.multiple_of(side * half, half), half)
                        copy = pltpu.make_async_copy(
                            stage.at[pl.ds(done * depth, depth), lanes],
                            to.at[meta[KEEP + which, done]],
                            sems.at[which, done],
                        )
                        copy.start()
                        copies.append(copy)
                    done += 1
    for copy in copies:
        copy.wait()


def grad_two_kernel(meta, earlier, current, dout, keep, send, stage, sems):
    frames, rows, width, chans = dout.shape

    def value_rows(a, b):
        return jnp.stack([frame_of(earlier, current, t + a, slice(b, b + rows)) for t in range(frames)])

    grads = dout[...].reshape(frames * rows, width, chans)
    weight_grad(meta, value_rows, grads, frames, rows, width, chans, stage, keep, send, sems)


def grad_one_kernel(
    meta, current, later, slope, earlier_clip, clip, near, far, near_o, far_o, keep, send, weights, stage, sems, out_sems
):
    copies = weight_copies(meta, (near, far, near_o, far_o), weights, sems)
    for copy in copies:
        copy.start()
    for copy in copies:
        copy.wait()
    frames, rows, width, chans = slope.shape
    parts = []
    for t in range(frames):
        back = conv_block(
            lambda a, b: frame_of(current, later, t + 2 - a, slice(2 - b, 2 - b + rows)), weights, chans, False
        )
        parts.append((back * slope[t]).astype(BF16))
    grads = jnp.concatenate(parts, axis=0)

    def value_rows(a, b):
        return jnp.stack(
            [frame_of(earlier_clip, clip, t + a, slice(b + 1, b + 1 + rows)) for t in range(frames)]
        )

    weight_grad(meta, value_rows, grads, frames, rows, width, chans, stage, keep, send, out_sems)


VM = pl.BlockSpec(memory_space=pltpu.VMEM)
HB = pl.BlockSpec(memory_space=pl.ANY)
SM = pl.BlockSpec(memory_space=pltpu.SMEM)


def call(kernel, name, ins, outs, out_shape, scratch):
    return pl.pallas_call(
        kernel,
        name=name,
        in_specs=ins,
        out_specs=outs,
        out_shape=out_shape,
        scratch_shapes=scratch,
        compiler_params=pltpu.CompilerParams(vmem_limit_bytes=VMEM_LIMIT),
    )


def shards(clip, teacher, kernel_one, kernel_two):
    frames_n, height_n, width_n, chans = clip.shape
    frames_axis, blocks = lax.axis_size("tm"), lax.axis_size("height")
    assert frames_axis & (frames_axis - 1) == 0 and frames_axis >= 2, "tm size"
    assert frames_n >= 2 and height_n >= 2, "block size"
    depth, half = kernel_one.shape[0], chans // 2
    place = lax.axis_index("height")
    core = lax.axis_index("tm") % 2

    orders = step_bits(blocks)
    masks = [relative_masks(order) for order in orders]
    inverse = [[mask.index(g) for g in range(blocks)] for mask in masks]
    ids = jnp.arange(blocks, dtype=jnp.int32)
    mask_table = jnp.array(masks, jnp.int32)
    inverse_table = jnp.array(inverse, jnp.int32)
    away = jnp.bitwise_xor(ids, place)
    info = jnp.where(ids == 0, core, jnp.where(ids == 1, place == 0, place == blocks - 1)).astype(jnp.int32)
    meta = jnp.stack(
        [
            jnp.bitwise_xor(mask_table[core], place),
            jnp.bitwise_xor(mask_table[1 - core], place),
            inverse_table[core][away],
            inverse_table[1 - core][away],
            info,
        ]
    )

    one = gather_kernel(kernel_one, core)
    two = gather_kernel(kernel_two, core)

    above = shifted(clip[:, height_n - 2 :], "height", 1)
    below = shifted(clip[:, :2], "height", -1)
    clip_ext = jnp.concatenate([above, clip, below], axis=1)
    clip_before = shifted(clip_ext[frames_n - 2 :], "tm", 1)

    weights = pltpu.VMEM((depth * blocks, chans), BF16)
    weight_sems = pltpu.SemaphoreType.DMA((2, blocks))
    block = (frames_n, height_n, width_n, chans)
    hidden, slope = call(
        conv_one_kernel,
        "conv_one",
        [SM, VM, VM] + [HB] * 4,
        [VM, VM],
        [
            jax.ShapeDtypeStruct((frames_n, height_n + 2, width_n, chans), BF16),
            jax.ShapeDtypeStruct(block, F32),
        ],
        [weights, weight_sems],
    )(meta, clip_before, clip_ext, *one)

    hidden_before = shifted(hidden[frames_n - 2 :], "tm", 1)
    count_all = frames_n * frames_axis * height_n * blocks * width_n
    student, dout = call(
        functools.partial(conv_two_kernel, 1.0 / math.sqrt(count_all)),
        "conv_two",
        [SM, VM, VM, VM, VM] + [HB] * 4,
        [VM, VM],
        [jax.ShapeDtypeStruct(block, BF16)] * 2,
        [weights, weight_sems],
    )(meta, hidden_before, hidden, clip, teacher, *two)

    d_above = shifted(dout[:, height_n - 1 :], "height", 1)
    d_below = shifted(dout[:, :1], "height", -1)

    grad_shape = jax.ShapeDtypeStruct((blocks, depth, half), BF16)
    keep_two, send_two = call(
        grad_two_kernel,
        "grad_two",
        [SM, VM, VM, VM],
        [HB, HB],
        [grad_shape] * 2,
        [weights, weight_sems],
    )(meta, hidden_before, hidden, dout)
    grad_two = scatter_grad(keep_two, send_two, core)

    dout_ext = jnp.concatenate([d_above, dout, d_below], axis=1)
    dout_after = shifted(dout_ext[:2], "tm", -1)
    keep_one, send_one = call(
        grad_one_kernel,
        "grad_one",
        [SM] + [VM] * 5 + [HB] * 4,
        [HB, HB],
        [grad_shape] * 2,
        [weights, weights, weight_sems, weight_sems],
    )(meta, dout_ext, dout_after, slope, clip_before, clip_ext, *two)
    grad_one = scatter_grad(keep_one, send_one, core)
    return (student, grad_one, grad_two)


def solution(mesh):
    in_specs = (
        P("tm", "height", None, None),
        P("tm", "height", None, None),
        P("height", None),
        P("height", None),
    )
    out_specs = (P("tm", "height", None, None), P("height", None), P("height", None))
    return jax.shard_map(shards, mesh=mesh, in_specs=in_specs, out_specs=out_specs, check_vma=False)
```

```python
import functools
import math

import jax
import jax.numpy as jnp
from jax import lax
from jax.experimental import pallas as pl
from jax.experimental.pallas import tpu as pltpu
from jax.sharding import PartitionSpec as P


BOTH = ("tm", "height")
BF16 = jnp.bfloat16
F32 = jnp.float32
VMEM_LIMIT = 56 * 1024 * 1024
TAPS = 3


def step_bits(blocks):
    bits = blocks.bit_length() - 1
    assert 1 << bits == blocks and bits >= 4, "height size"
    high = list(range(bits - 1, 1, -1))
    return high + [0, 1], [high[1], high[0]] + high[2:] + [1, 0]


def relative_masks(order):
    return [sum(((r >> k) & 1) << bit for k, bit in enumerate(order)) for r in range(1 << len(order))]


def step_pairs(frames_axis, blocks, step):
    orders = step_bits(blocks)
    return [
        (t * blocks + h, t * blocks + (h ^ (1 << orders[t % 2][step])))
        for t in range(frames_axis)
        for h in range(blocks)
    ]


def shifted(value, axis, by):
    count = lax.axis_size(axis)
    return lax.ppermute(value, axis, [(i, i + by) for i in range(count) if 0 <= i + by < count])


def stepped(value, step):
    return lax.ppermute(value, BOTH, step_pairs(lax.axis_size("tm"), lax.axis_size("height"), step))


def swapped(value, group=1):
    return lax.ppermute(value, "tm", [(t, t ^ group) for t in range(lax.axis_size("tm"))])


def gather_kernel(shard, core):
    half = shard.shape[1] // 2
    steps = lax.axis_size("height").bit_length() - 1
    near = lax.dynamic_slice(shard, (0, core * half), (shard.shape[0], half))[None]
    for step in range(steps - 1):
        near = jnp.concatenate([near, stepped(near, step)], axis=0)
    far = stepped(near, steps - 1)
    return near, far, swapped(near), swapped(far)


def total(first, second):
    return first.astype(F32) + second.astype(F32)


def scatter_grad(keep, send, core):
    frames_axis, blocks = lax.axis_size("tm"), lax.axis_size("height")
    here, came = keep, swapped(send)
    count = blocks
    for step in reversed(range(blocks.bit_length() - 1)):
        count //= 2
        got = stepped(total(here[count:], came[count:]).astype(BF16), step)
        here = total(here[:count], came[:count])
        if count > 4:
            here = here.astype(BF16)
        came = got
    own = total(here[0], came[0])
    group = 2
    while group < frames_axis:
        own = total(own, swapped(own, group))
        group *= 2
    other = swapped(own)
    first = jnp.where(core == 0, own, other)
    second = jnp.where(core == 0, other, own)
    return jnp.concatenate([first, second], axis=1)


def column_shift(value, by):
    width = value.shape[1]
    cols = lax.broadcasted_iota(jnp.int32, value.shape, 1)
    rolled = pltpu.roll(value, by % width, 1)
    return jnp.where((cols < by) if by > 0 else (cols >= width + by), 0.0, rolled)


def chunk_tables(blocks):
    masks = [relative_masks(order) for order in step_bits(blocks)]
    return masks, [[mask.index(g) for g in range(blocks)] for mask in masks]


def weight_copies(parts, whole, sems):
    near, far, near_other, far_other = parts
    count, rows, half = near.shape
    core, place = lax.axis_index("tm") & 1, lax.axis_index("height")
    masks, _ = chunk_tables(2 * count)
    for which, (low, high, side) in enumerate(((near, far, core), (near_other, far_other, 1 - core))):
        lanes = pl.ds(pl.multiple_of(side * half, half), half)
        for r in range(2 * count):
            source = (low if r < count else high).at[r % count]
            owner = place ^ jnp.where(side == 0, masks[0][r], masks[1][r])
            pltpu.make_async_copy(
                source, whole.at[pl.ds(pl.multiple_of(owner * rows, rows), rows), lanes], sems.at[which, owner]
            ).start()


def weight_wait(parts, whole, sems, until, done):
    near = parts[0]
    count, rows, half = near.shape
    while done * rows < until and done < 2 * count:
        for which in range(2):
            pltpu.make_async_copy(
                near.at[0], whole.at[pl.ds(done * rows, rows), pl.ds(which * half, half)], sems.at[which, done]
            ).wait()
        done += 1
    return done


def tap_rows(chans, a, b, c):
    first = ((a * TAPS + b) * TAPS + c) * chans
    return slice(first, first + chans)


def stacked_rows(earlier, current, at, frames, rows):
    held = earlier.shape[0]
    pieces = [earlier[t, rows] if t < held else current[t - held, rows] for t in range(at, at + frames)]
    return jnp.concatenate(pieces, axis=0)


def convolve(slab, parts, weights, sums, sems, forward):
    weight_copies(parts, weights, sems)
    done = 0
    for a in range(TAPS):
        for b in range(TAPS):
            value = slab(a, b)
            rows, width, chans = value.shape
            value = value.reshape(rows * width, chans)
            for c in range(TAPS):
                at = tap_rows(chans, a, b, c)
                done = weight_wait(parts, weights, sems, at.stop, done)
                part = lax.dot_general(
                    value, weights[at, :], (((1,), (0 if forward else 1,)), ((), ())), preferred_element_type=F32
                )
                sums[c] = part if a == b == 0 else sums[c] + part
    moved = [sums[c].reshape(rows, width, chans) for c in range(TAPS)]
    by = 1 if forward else -1
    return column_shift(moved[0], by) + moved[1] + column_shift(moved[2], -by)


def conv_one_kernel(earlier, current, near, far, near_o, far_o, hidden, slope, weights, sums, sems):
    frames, rows, width, chans = hidden.shape
    pre = convolve(
        lambda a, b: stacked_rows(earlier, current, a, frames, slice(b, b + rows)),
        (near, far, near_o, far_o), weights, sums, sems, True,
    ).reshape(frames, rows, width, chans)
    gate = 1.0 / (1.0 + jnp.exp(-pre))
    value = (pre * gate).astype(BF16)
    place = lax.axis_index("height")
    row = lax.broadcasted_iota(jnp.int32, value.shape, 1)
    cut = jnp.logical_or(
        jnp.logical_and(row == 0, place == 0),
        jnp.logical_and(row == rows - 1, place == lax.axis_size("height") - 1),
    )
    hidden[...] = jnp.where(cut, jnp.zeros_like(value), value)
    slope[...] = (gate * (1.0 + pre * (1.0 - gate)))[:, 1 : rows - 1]


def conv_two_kernel(
    factor, earlier, current, clip, teacher, near, far, near_o, far_o, student, dout, weights, sums, sems
):
    frames, rows, width, chans = student.shape
    branch = convolve(
        lambda a, b: stacked_rows(earlier, current, a, frames, slice(b, b + rows)),
        (near, far, near_o, far_o), weights, sums, sems, True,
    ).reshape(frames, rows, width, chans)
    output = clip[...].astype(F32) + branch
    student[...] = output.astype(BF16)
    dout[...] = ((output - teacher[...].astype(F32)) * factor).astype(BF16)


def dpre_kernel(current, later, slope, near, far, near_o, far_o, dpre, weights, sums, sems):
    frames, rows, width, chans = dpre.shape
    back = convolve(
        lambda a, b: stacked_rows(current, later, 2 - a, frames, slice(2 - b, 2 - b + rows)),
        (near, far, near_o, far_o), weights, sums, sems, False,
    ).reshape(frames, rows, width, chans)
    dpre[...] = (back * slope[...]).astype(BF16)


def weight_grad_kernel(margin, earlier, current, grads, keep, send, stage, sems):
    frames, rows, width, chans = grads.shape
    size = frames * rows * width
    near = grads[...].reshape(frames * rows, width, chans)
    wide = near.astype(F32)
    moved = [
        (column_shift(wide, c - 1).astype(BF16) if c != 1 else near).reshape(size, chans) for c in range(TAPS)
    ]
    count, depth, half = keep.shape
    core, place = lax.axis_index("tm") & 1, lax.axis_index("height")
    _, places = chunk_tables(count)
    copies = []
    done = 0
    for a in range(TAPS):
        for b in range(TAPS):
            value = stacked_rows(earlier, current, a, frames, slice(b + margin, b + margin + rows))
            turned = value.reshape(size, chans).T
            for c in range(TAPS):
                at = tap_rows(chans, a, b, c)
                stage[at, :] = jnp.dot(turned, moved[c], preferred_element_type=F32).astype(BF16)
                while (done + 1) * depth <= at.stop and done < count:
                    for which, (to, side) in enumerate(((keep, core), (send, 1 - core))):
                        lanes = pl.ds(pl.multiple_of(side * half, half), half)
                        target = jnp.where(side == 0, places[0][done], places[1][done]) ^ position(place, side)
                        copy = pltpu.make_async_copy(
                            stage.at[pl.ds(done * depth, depth), lanes], to.at[target], sems.at[which, done]
                        )
                        copy.start()
                        copies.append(copy)
                    done += 1
    for copy in copies:
        copy.wait()


def position(place, side):
    blocks = lax.axis_size("height")
    result = 0
    for first, second in zip(*(enumerate_bits(order) for order in step_bits(blocks))):
        bit0 = ((place >> first[1]) & 1) << first[0]
        bit1 = ((place >> second[1]) & 1) << second[0]
        result = result | jnp.where(side == 0, bit0, bit1)
    return result


def enumerate_bits(order):
    return list(enumerate(order))


VM = pl.BlockSpec(memory_space=pltpu.VMEM)
HB = pl.BlockSpec(memory_space=pl.ANY)


def call(kernel, ins, outs, out_shape, scratch):
    return pl.pallas_call(
        kernel,
        in_specs=ins,
        out_specs=outs,
        out_shape=out_shape,
        scratch_shapes=scratch,
        compiler_params=pltpu.CompilerParams(vmem_limit_bytes=VMEM_LIMIT),
    )


def step(clip, teacher, kernel_one, kernel_two):
    frames_n, height_n, width_n, chans = clip.shape
    frames_axis, blocks = lax.axis_size("tm"), lax.axis_size("height")
    assert frames_axis & (frames_axis - 1) == 0 and frames_axis >= 2, "tm size"
    assert frames_n >= 2 and height_n >= 2, "block size"
    depth, half = kernel_one.shape[0], chans // 2
    core = lax.axis_index("tm") & 1

    one = gather_kernel(kernel_one, core)
    two = gather_kernel(kernel_two, core)

    above = shifted(clip[:, height_n - 2 :], "height", 1)
    below = shifted(clip[:, :2], "height", -1)
    clip_ext = jnp.concatenate([above, clip, below], axis=1)
    clip_before = shifted(clip_ext[frames_n - 2 :], "tm", 1)

    weights = pltpu.VMEM((depth * blocks, chans), BF16)
    weight_sems = pltpu.SemaphoreType.DMA((2, blocks))
    block = (frames_n, height_n, width_n, chans)

    def sums(rows):
        return pltpu.VMEM((TAPS, frames_n * rows * width_n, chans), F32)

    hidden, slope = call(
        conv_one_kernel,
        [VM, VM] + [HB] * 4,
        [VM, VM],
        [
            jax.ShapeDtypeStruct((frames_n, height_n + 2, width_n, chans), BF16),
            jax.ShapeDtypeStruct(block, F32),
        ],
        [weights, sums(height_n + 2), weight_sems],
    )(clip_before, clip_ext, *one)

    hidden_before = shifted(hidden[frames_n - 2 :], "tm", 1)
    count_all = frames_n * frames_axis * height_n * blocks * width_n
    student, dout = call(
        functools.partial(conv_two_kernel, 1.0 / math.sqrt(count_all)),
        [VM] * 4 + [HB] * 4,
        [VM, VM],
        [jax.ShapeDtypeStruct(block, BF16)] * 2,
        [weights, sums(height_n), weight_sems],
    )(hidden_before, hidden, clip, teacher, *two)

    d_above = shifted(dout[:, height_n - 1 :], "height", 1)
    d_below = shifted(dout[:, :1], "height", -1)

    grad_shape = jax.ShapeDtypeStruct((blocks, depth, half), BF16)

    def weight_grad(margin, earlier, current, grads):
        return call(
            functools.partial(weight_grad_kernel, margin),
            [VM, VM, VM],
            [HB, HB],
            [grad_shape] * 2,
            [weights, weight_sems],
        )(earlier, current, grads)

    keep_two, send_two = weight_grad(0, hidden_before, hidden, dout)
    grad_two = scatter_grad(keep_two, send_two, core)

    dout_ext = jnp.concatenate([d_above, dout, d_below], axis=1)
    dout_after = shifted(dout_ext[:2], "tm", -1)
    dpre = call(
        dpre_kernel, [VM] * 3 + [HB] * 4, VM, jax.ShapeDtypeStruct(block, BF16), [weights, sums(height_n), weight_sems]
    )(dout_ext, dout_after, slope, *two)
    keep_one, send_one = weight_grad(1, clip_before, clip_ext, dpre)
    grad_one = scatter_grad(keep_one, send_one, core)
    return (student, grad_one, grad_two)


def solution(mesh):
    in_specs = (
        P("tm", "height", None, None),
        P("tm", "height", None, None),
        P("height", None),
        P("height", None),
    )
    out_specs = (P("tm", "height", None, None), P("height", None), P("height", None))
    return jax.shard_map(step, mesh=mesh, in_specs=in_specs, out_specs=out_specs, check_vma=False)
```

```python
import functools
import math

import jax
import jax.numpy as jnp
from jax import lax
from jax.experimental import pallas as pl
from jax.experimental.pallas import tpu as pltpu
from jax.sharding import PartitionSpec as P


BOTH = ("tm", "height")
BF16 = jnp.bfloat16
F32 = jnp.float32
VMEM_LIMIT = 24 * 1024 * 1024
TAPS = 3


def step_bits(blocks, late):
    bits = blocks.bit_length() - 1
    assert 1 << bits == blocks and bits >= 4, "height size"
    high = list(range(bits - 1, 1, -1))
    swap = [high[1], high[0]] + high[2:]
    if late:
        return high + [0, 1], swap + [1, 0]
    return [0] + high + [1], [1] + swap + [0]


def relative_masks(order):
    return [sum(((r >> k) & 1) << bit for k, bit in enumerate(order)) for r in range(1 << len(order))]


def step_pairs(frames_axis, blocks, step, late):
    orders = step_bits(blocks, late)
    return [
        (t * blocks + h, t * blocks + (h ^ (1 << orders[t % 2][step])))
        for t in range(frames_axis)
        for h in range(blocks)
    ]


def shifted(value, axis, by):
    count = lax.axis_size(axis)
    return lax.ppermute(value, axis, [(i, i + by) for i in range(count) if 0 <= i + by < count])


def stepped(value, step, late):
    return lax.ppermute(value, BOTH, step_pairs(lax.axis_size("tm"), lax.axis_size("height"), step, late))


def swapped(value, group=1):
    return lax.ppermute(value, "tm", [(t, t ^ group) for t in range(lax.axis_size("tm"))])


def gather_kernel(shard, core, late):
    half = shard.shape[1] // 2
    steps = lax.axis_size("height").bit_length() - 1
    near = lax.dynamic_slice(shard, (0, core * half), (shard.shape[0], half))[None]
    for step in range(steps - 1):
        near = jnp.concatenate([near, stepped(near, step, late)], axis=0)
    far = stepped(near, steps - 1, late)
    return near, far, swapped(near), swapped(far)


def total(first, second):
    return first.astype(F32) + second.astype(F32)


def scatter_grad(keep, send, core, late):
    frames_axis, blocks = lax.axis_size("tm"), lax.axis_size("height")
    here, came = keep, swapped(send)
    count = blocks
    for step in reversed(range(blocks.bit_length() - 1)):
        count //= 2
        got = stepped(total(here[count:], came[count:]).astype(BF16), step, late)
        here = total(here[:count], came[:count])
        if count > 4:
            here = here.astype(BF16)
        came = got
    own = total(here[0], came[0])
    group = 2
    while group < frames_axis:
        own = total(own, swapped(own, group))
        group *= 2
    other = swapped(own)
    first = jnp.where(core == 0, own, other)
    second = jnp.where(core == 0, other, own)
    return jnp.concatenate([first, second], axis=1)


def column_shift(value, by):
    width = value.shape[1]
    cols = lax.broadcasted_iota(jnp.int32, value.shape, 1)
    rolled = pltpu.roll(value, by % width, 1)
    return jnp.where((cols < by) if by > 0 else (cols >= width + by), 0.0, rolled)


def chunk_tables(blocks, late):
    masks = [relative_masks(order) for order in step_bits(blocks, late)]
    return masks, [[mask.index(g) for g in range(blocks)] for mask in masks]


def weight_copies(parts, whole, sems, late):
    near, far, near_other, far_other = parts
    count, rows, half = near.shape
    core, place = lax.axis_index("tm") & 1, lax.axis_index("height")
    masks, _ = chunk_tables(2 * count, late)
    for which, (low, high, side) in enumerate(((near, far, core), (near_other, far_other, 1 - core))):
        lanes = pl.ds(pl.multiple_of(side * half, half), half)
        for r in range(2 * count):
            source = (low if r < count else high).at[r % count]
            owner = place ^ jnp.where(side == 0, masks[0][r], masks[1][r])
            pltpu.make_async_copy(
                source, whole.at[pl.ds(pl.multiple_of(owner * rows, rows), rows), lanes], sems.at[which, owner]
            ).start()


def weight_wait(parts, whole, sems, until, done):
    near = parts[0]
    count, rows, half = near.shape
    while done * rows < until and done < 2 * count:
        for which in range(2):
            pltpu.make_async_copy(
                near.at[0], whole.at[pl.ds(done * rows, rows), pl.ds(which * half, half)], sems.at[which, done]
            ).wait()
        done += 1
    return done


def tap_rows(chans, a, b, c):
    first = ((a * TAPS + b) * TAPS + c) * chans
    return slice(first, first + chans)


def stacked_rows(earlier, current, at, frames, rows):
    held = earlier.shape[0]
    pieces = [earlier[t, rows] if t < held else current[t - held, rows] for t in range(at, at + frames)]
    return jnp.concatenate(pieces, axis=0)


def convolve(slab, parts, weights, sems, forward, late):
    weight_copies(parts, weights, sems, late)
    order = [(a, b) for a in range(TAPS) for b in range(TAPS)]
    pieces = [slab(a, b) for a, b in order]
    rows, width, chans = pieces[0].shape
    left = jnp.concatenate([piece.reshape(rows * width, chans) for piece in pieces], axis=1)
    weight_wait(parts, weights, sems, weights.shape[0], 0)
    result = None
    for c in range(TAPS):
        blocks = [weights[tap_rows(chans, a, b, c), :] for a, b in order]
        right = jnp.concatenate(blocks, axis=0 if forward else 1)
        part = lax.dot_general(
            left, right, (((1,), (0 if forward else 1,)), ((), ())), preferred_element_type=F32
        ).reshape(rows, width, chans)
        by = (1 - c) if forward else (c - 1)
        if by:
            part = column_shift(part, by)
        result = part if result is None else result + part
    return result


def outside(shape, margin):
    place = lax.axis_index("height")
    row = lax.broadcasted_iota(jnp.int32, shape, 1)
    first = jnp.where(place == 0, margin, 0)
    stop = jnp.where(place == lax.axis_size("height") - 1, shape[1] - margin, shape[1])
    return jnp.logical_or(row < first, row >= stop)


def conv_one_kernel(late, earlier, current, near, far, near_o, far_o, hidden, slope, weights, sems):
    frames, rows, width, chans = hidden.shape
    margin = (rows - slope.shape[1]) // 2
    pre = convolve(
        lambda a, b: stacked_rows(earlier, current, a, frames, slice(b, b + rows)),
        (near, far, near_o, far_o), weights, sems, True, late,
    ).reshape(frames, rows, width, chans)
    gate = 1.0 / (1.0 + jnp.exp(-pre))
    value = (pre * gate).astype(BF16)
    hidden[...] = jnp.where(outside(value.shape, margin), jnp.zeros_like(value), value)
    inner = slice(margin, rows - margin)
    gate, pre = gate[:, inner], pre[:, inner]
    slope[...] = gate * (1.0 + pre * (1.0 - gate))


def conv_two_kernel(
    factor, late, earlier, current, clip, teacher, near, far, near_o, far_o, student, dout, weights, sems
):
    frames, rows, width, chans = dout.shape
    margin = (rows - student.shape[1]) // 2
    skip = (clip.shape[1] - rows) // 2
    branch = convolve(
        lambda a, b: stacked_rows(earlier, current, a, frames, slice(b, b + rows)),
        (near, far, near_o, far_o), weights, sems, True, late,
    ).reshape(frames, rows, width, chans)
    output = clip[:, skip : skip + rows].astype(F32) + branch
    student[...] = output[:, margin : rows - margin].astype(BF16)
    value = ((output - teacher[...].astype(F32)) * factor).astype(BF16)
    dout[...] = jnp.where(outside(value.shape, margin), jnp.zeros_like(value), value)


def dpre_kernel(late, current, later, slope, near, far, near_o, far_o, dpre, weights, sems):
    frames, rows, width, chans = dpre.shape
    back = convolve(
        lambda a, b: stacked_rows(current, later, 2 - a, frames, slice(2 - b, 2 - b + rows)),
        (near, far, near_o, far_o), weights, sems, False, late,
    ).reshape(frames, rows, width, chans)
    dpre[...] = (back * slope[...]).astype(BF16)


def weight_grad_kernel(late, inner, earlier, current, grads, keep, send):
    frames, rows, width, chans = grads.shape
    rows -= 2 * inner
    count, depth, half = keep.shape
    margin = (current.shape[1] - rows) // 2
    size = frames * rows * width
    near = grads[:, inner : inner + rows].reshape(frames * rows, width, chans)
    wide = near.astype(F32)
    moved = [
        (column_shift(wide, c - 1).astype(BF16) if c != 1 else near).reshape(size, chans) for c in range(TAPS)
    ]
    core, place = lax.axis_index("tm") & 1, lax.axis_index("height")
    _, places = chunk_tables(count, late)
    base = [position(place, side, late) for side in (core, 1 - core)]
    for a in range(TAPS):
        for b in range(TAPS):
            first = b + margin - 1
            value = stacked_rows(earlier, current, a, frames, slice(first, first + rows))
            turned = value.reshape(size, chans).T
            for c in range(TAPS):
                at = tap_rows(chans, a, b, c)
                part = jnp.dot(turned, moved[c], preferred_element_type=F32).astype(BF16)
                left, right = part[:, :half], part[:, half:]
                mine = jnp.where(core == 0, left, right)
                theirs = jnp.where(core == 0, right, left)
                start = at.start
                while start < at.stop:
                    chunk = start // depth
                    stop = min(at.stop, (chunk + 1) * depth)
                    here = slice(start - chunk * depth, stop - chunk * depth)
                    there = slice(start - at.start, stop - at.start)
                    for to, block, side, shift in ((keep, mine, core, base[0]), (send, theirs, 1 - core, base[1])):
                        target = jnp.where(side == 0, places[0][chunk], places[1][chunk]) ^ shift
                        to[target, here, :] = block[there]
                    start = stop


def position(place, side, late):
    result = 0
    for k, (bit0, bit1) in enumerate(zip(*step_bits(lax.axis_size("height"), late))):
        result = result | jnp.where(side == 0, ((place >> bit0) & 1) << k, ((place >> bit1) & 1) << k)
    return result


VM = pl.BlockSpec(memory_space=pltpu.VMEM)
HB = pl.BlockSpec(memory_space=pl.ANY)


def call(kernel, ins, outs, out_shape, scratch):
    return pl.pallas_call(
        kernel,
        in_specs=ins,
        out_specs=outs,
        out_shape=out_shape,
        scratch_shapes=scratch,
        compiler_params=pltpu.CompilerParams(vmem_limit_bytes=VMEM_LIMIT),
    )


def step(clip, teacher, kernel_one, kernel_two):
    frames_n, height_n, width_n, chans = clip.shape
    frames_axis, blocks = lax.axis_size("tm"), lax.axis_size("height")
    assert frames_axis & (frames_axis - 1) == 0 and frames_axis >= 2, "tm size"
    assert frames_n >= 2 and height_n >= 3, "block size"
    depth, half = kernel_one.shape[0], chans // 2
    core = lax.axis_index("tm") & 1

    one = gather_kernel(kernel_one, core, True)
    two = gather_kernel(kernel_two, core, False)

    last_rows = jnp.concatenate([clip[:, height_n - 3 :], teacher[:, height_n - 1 :]], axis=1)
    first_rows = jnp.concatenate([clip[:, :3], teacher[:, :1]], axis=1)
    above = shifted(last_rows, "height", 1)
    below = shifted(first_rows, "height", -1)
    clip_ext = jnp.concatenate([above[:, :3], clip, below[:, :3]], axis=1)
    teacher_ext = jnp.concatenate([above[:, 3:], teacher, below[:, 3:]], axis=1)
    clip_before = shifted(clip_ext[frames_n - 2 :], "tm", 1)

    weights = pltpu.VMEM((depth * blocks, chans), BF16)
    scratch = [weights, pltpu.SemaphoreType.DMA((2, blocks))]

    def block(margin, kind=BF16):
        return jax.ShapeDtypeStruct((frames_n, height_n + 2 * margin, width_n, chans), kind)

    hidden, slope = call(
        functools.partial(conv_one_kernel, True), [VM, VM] + [HB] * 4, [VM, VM], [block(2), block(0, F32)], scratch
    )(clip_before, clip_ext, *one)

    hidden_before = shifted(hidden[frames_n - 2 :], "tm", 1)
    count_all = frames_n * frames_axis * height_n * blocks * width_n
    student, dout = call(
        functools.partial(conv_two_kernel, 1.0 / math.sqrt(count_all), False),
        [VM] * 4 + [HB] * 4, [VM, VM], [block(0), block(1)], scratch,
    )(hidden_before, hidden, clip_ext, teacher_ext, *two)

    dout_after = shifted(dout[:2], "tm", -1)

    grad_shape = jax.ShapeDtypeStruct((blocks, depth, half), BF16)

    def weight_grad(late, inner, earlier, current, grads):
        return call(
            functools.partial(weight_grad_kernel, late, inner), [VM] * 3, [VM] * 2, [grad_shape] * 2, []
        )(earlier, current, grads)

    keep_two, send_two = weight_grad(False, 1, hidden_before, hidden, dout)
    grad_two = scatter_grad(keep_two, send_two, core, False)

    dpre = call(
        functools.partial(dpre_kernel, False), [VM] * 3 + [HB] * 4, VM, block(0), scratch
    )(dout, dout_after, slope, *two)
    keep_one, send_one = weight_grad(True, 0, clip_before, clip_ext, dpre)
    grad_one = scatter_grad(keep_one, send_one, core, True)
    return (student, grad_one, grad_two)


def solution(mesh):
    in_specs = (
        P("tm", "height", None, None),
        P("tm", "height", None, None),
        P("height", None),
        P("height", None),
    )
    out_specs = (P("tm", "height", None, None), P("height", None), P("height", None))
    return jax.shard_map(step, mesh=mesh, in_specs=in_specs, out_specs=out_specs, check_vma=False)
```
